256 devices in a mesh: sec: 4 (over x_hi, core), ctx: 64 (over y, x_lo, z).
Axes of the slice: x: 4 (x_hi: 2, x_lo: 2; x = x_hi * 2 + x_lo), y: 4, z: 8, core: 2. Of those that a mesh axis runs over, the one named last changes fastest.
Arguments:
- queries: bfloat16 [4, 128, 64, 4096], P('sec', 'ctx'), may hold values from -6 to 6
- head_weights: float32 [4, 128, 64, 32], P('sec', 'ctx'), may hold values from -0.9 to 0.9
- key_vectors: bfloat16 [4, 524288, 128], P('sec', 'ctx'), may hold values from -6 to 6
- targets: bfloat16 [4, 128, 64, 4096], P('sec', 'ctx'), may hold values from 0 to 0.0019989014
- normalizers: float32 [4, 128, 64], P('sec', 'ctx'), may hold values from 7 to 9
- loss_grad: float32 [4, 128, 64], P('sec', 'ctx'), may hold values from 300 to 3000
- tile_slot: int32 [4, 128], P('sec', 'ctx'), may hold values from 0 to 127
- doc_start: int32 [4, 128], P('sec', 'ctx'), may hold values from 0 to 524287, as said below
Outputs:
- queries_grad: bfloat16 [4, 128, 64, 4096], P('sec', 'ctx')
- weights_grad: float32 [4, 128, 64, 32], P('sec', 'ctx')
- key_grads: bfloat16 [4, 524288, 128], P('sec', 'ctx')
The draws below stay inside these ranges and needn't reach their ends.
Inputs may be any that keep to these rules, and one draw needn't show every extreme that they name: `doc_start`: qpos of every task lies in its device's positions; the document of a task starts at or before its first query and spans 1 to 4 key blocks up to its last query; the first task of every device but the first spans 4 blocks and its document starts on the device before.
All inputs are finite; a program needn't handle non-finite values.
Results may differ from the reference program's by a relative error of at most 0.0051.
Values may be sent and summed in bfloat16 or wider, within the bound.
A program may use at most 192 MiB of HBM per device.

```python
import math
import jax
import jax.numpy as jnp
from jax import lax

H = 32
DH = 128
BLK = 1024
MAXB = 4
QT = 64
TASK_DEV = 2
KB_DEV = 8
SEQS = 4
NTASK = 128
SEQ = 524288


def task_layout(key):
    base = jax.random.fold_in(key, 7103)
    keys_list = jax.random.split(base, 4)
    shape_pair = (SEQS, NTASK)
    task_ids = jnp.arange(NTASK, dtype=jnp.int32)[None, :] + jnp.zeros(shape_pair, jnp.int32)
    device_ids = task_ids // TASK_DEV
    crossing = (task_ids % TASK_DEV == 0) & (device_ids > 0)
    free_block = jax.random.randint(keys_list[0], shape_pair, 0, KB_DEV)
    cross_block = jax.random.randint(keys_list[1], shape_pair, 0, MAXB - 1)
    local_block = jnp.where(crossing, cross_block, free_block)
    per_block = BLK // QT
    within = jax.random.randint(keys_list[2], shape_pair, 0, per_block)
    slot_value = local_block * per_block + within
    free_back = jax.random.randint(keys_list[3], shape_pair, 0, MAXB)
    back_blocks = jnp.where(crossing, MAXB - 1, free_back)
    last_block = device_ids * KB_DEV + local_block
    first_block = jnp.maximum(last_block - back_blocks, 0)
    query_first = last_block * BLK + within * QT
    span = jnp.minimum(BLK, query_first - first_block * BLK + 1)
    offset = jax.random.randint(jax.random.fold_in(base, 11), shape_pair, 0, 1 << 20) % span
    doc_begin = first_block * BLK + offset
    return (slot_value.astype(jnp.int32), doc_begin.astype(jnp.int32))


def draw_tile_slot(key, part):
    return task_layout(key)[0]


def draw_doc_start(key, part):
    return task_layout(key)[1]


def steps_of(own_key, dims, cuts, least, high):
    def one(dim, shards_of):
        heights = jax.random.uniform(jax.random.fold_in(jax.random.fold_in(own_key, 6), dim), (shards_of,), jnp.float32, least / len(cuts), high / len(cuts))
        return jnp.repeat(jnp.exp(heights), dims[dim] // shards_of).reshape((-1,) + (1,) * (len(dims) - dim - 1))

    factor_of = one(*cuts[0])
    for cut in cuts[1:]:
        factor_of = factor_of * one(*cut)
    return factor_of


def gaussian(stream_key, shape, spread, limit, shards=(), kind=jnp.bfloat16):
    factor_of = steps_of(stream_key, shape, shards, -0.22, 0.18) if shards else 1.0
    drawn = jax.random.normal(stream_key, shape, jnp.float32) * spread * factor_of
    return jnp.minimum(jnp.maximum(drawn, -limit), limit).astype(kind)


def setup_inputs(seed: int = 0) -> dict:
    key_of = jax.random.split(jax.random.key(seed), 9)
    return {
        "queries": gaussian(key_of[0], (SEQS, NTASK, QT, H * DH), 1.0, 6.0, ((0, 4), (1, 64))),
        "head_weights": gaussian(key_of[1], (SEQS, NTASK, QT, H), 0.15, 0.9, ((0, 4), (1, 64)), jnp.float32),
        "key_vectors": gaussian(key_of[2], (SEQS, SEQ, DH), 1.0, 6.0, ((0, 4), (1, 64))),
        "targets": jnp.clip(0.0019989014 * jax.random.uniform(key_of[3], (SEQS, NTASK, QT, MAXB * BLK), jnp.float32) ** steps_of(key_of[3], (SEQS, NTASK, QT, MAXB * BLK), ((0, 4), (1, 64)), -0.2, 0.2), 0.0, 0.0019989014).astype(jnp.bfloat16),
        "normalizers": jnp.clip(7.0 + 2.0 * jax.random.uniform(key_of[4], (SEQS, NTASK, QT), jnp.float32) ** steps_of(key_of[4], (SEQS, NTASK, QT), ((0, 4), (1, 64)), -0.2, 0.2), 7.0, 9.0),
        "loss_grad": jnp.clip(jnp.exp(math.log(3000.0) - 2.3025851 * jax.random.uniform(key_of[5], (SEQS, NTASK, QT), jnp.float32) ** steps_of(key_of[5], (SEQS, NTASK, QT), ((0, 4), (1, 64)), -0.2, 0.2)), 300.0, 3000.0),
        "tile_slot": draw_tile_slot(jax.random.fold_in(key_of[8], 71), 0),
        "doc_start": draw_doc_start(jax.random.fold_in(key_of[8], 71), 0),
    }


def block_terms(query_rows, weight_rows, normalizer, cotangent, target_block, key_block, key_first, query_pos, doc_begin, inside):
    tile_rows = weight_rows.shape[0]
    head_count = weight_rows.shape[1]
    block_width = key_block.shape[0]
    factor = 1.0 / (key_block.shape[1] ** 0.5)
    scores = lax.dot_general(query_rows, key_block, (((1,), (1,)), ((), ())), preferred_element_type=jnp.float32)
    scores = scores.reshape(tile_rows, head_count, block_width)
    active = jnp.maximum(scores, 0.0) * factor
    index_value = jnp.sum(weight_rows[:, :, None] * active, axis=1)
    key_pos = key_first + jnp.arange(block_width, dtype=jnp.int32)
    live = (key_pos[None, :] >= doc_begin) & (key_pos[None, :] <= query_pos[:, None]) & inside
    delta = jnp.where(live, cotangent[:, None] * (jnp.exp(index_value - normalizer[:, None]) - target_block.astype(jnp.float32)), 0.0)
    weight_part = jnp.sum(delta[:, None, :] * active, axis=2)
    score_grad = jnp.where(scores > 0, delta[:, None, :] * weight_rows[:, :, None] * factor, 0.0).astype(jnp.bfloat16)
    score_grad = score_grad.reshape(tile_rows * head_count, block_width)
    query_part = jnp.dot(score_grad, key_block, preferred_element_type=jnp.float32)
    key_part = lax.dot_general(score_grad, query_rows, (((0,), (0,)), ((), ())), preferred_element_type=jnp.float32)
    return query_part, weight_part, key_part


def one_sequence(operands):
    queries, head_weights, key_vectors, targets, normalizers, loss_grad, tile_slot, doc_start = operands

    def one_task(key_state, task_items):
        task_index, query_tile, weight_rows, target_rows, normalizer, cotangent, slot_value, doc_begin = task_items
        query_rows = query_tile.reshape(QT * H, DH)
        query_first = (task_index // TASK_DEV) * (KB_DEV * BLK) + slot_value * QT
        query_pos = query_first + jnp.arange(QT, dtype=jnp.int32)
        first_block = doc_begin // BLK
        block_count = (query_first + QT - 1) // BLK - first_block + 1

        def per_slot(slot_index, carry):
            query_total, weight_total, own_sum, lent_sum = carry
            block_id = first_block + slot_index
            key_block = lax.dynamic_slice_in_dim(key_vectors, (block_id * BLK).astype(jnp.int32), BLK, 0)
            target_block = lax.dynamic_slice_in_dim(target_rows, (slot_index * BLK).astype(jnp.int32), BLK, 1)
            query_part, weight_part, key_part = block_terms(query_rows, weight_rows, normalizer, cotangent, target_block, key_block, block_id * BLK, query_pos, doc_begin, True)
            is_own = (block_id // KB_DEV) == (task_index // TASK_DEV)
            start = (block_id * BLK).astype(jnp.int32)
            prev_own = lax.dynamic_slice_in_dim(own_sum, start, BLK, 0)
            own_sum = lax.dynamic_update_slice_in_dim(own_sum, prev_own + jnp.where(is_own, key_part, 0.0), start, 0)
            prev_lent = lax.dynamic_slice_in_dim(lent_sum, start, BLK, 0)
            lent_sum = lax.dynamic_update_slice_in_dim(lent_sum, prev_lent + jnp.where(is_own, 0.0, key_part), start, 0)
            return query_total + query_part, weight_total + weight_part, own_sum, lent_sum

        start_state = (jnp.zeros((QT * H, DH), jnp.float32), jnp.zeros((QT, H), jnp.float32), key_state[0], key_state[1])
        query_total, weight_total, own_sum, lent_sum = lax.fori_loop(0, block_count, per_slot, start_state)
        return (own_sum, lent_sum), (query_total.reshape(QT, H * DH).astype(jnp.bfloat16), weight_total)

    key_start = (jnp.zeros((SEQ, DH), jnp.float32), jnp.zeros((SEQ, DH), jnp.float32))
    task_ids = jnp.arange(NTASK, dtype=jnp.int32)
    key_state, outputs = lax.scan(one_task, key_start, (task_ids, queries, head_weights, targets, normalizers, loss_grad, tile_slot, doc_start))
    lent_round = lax.optimization_barrier(key_state[1].astype(jnp.bfloat16))
    key_out = (key_state[0] + lent_round.astype(jnp.float32)).astype(jnp.bfloat16)
    return outputs[0], outputs[1], key_out


def reference(queries, head_weights, key_vectors, targets, normalizers, loss_grad, tile_slot, doc_start):
    query_out, weight_out, key_out = lax.map(one_sequence, (queries, head_weights, key_vectors, targets, normalizers, loss_grad, tile_slot, doc_start))
    return query_out, weight_out, key_out
```

```python
import jax
import jax.numpy as jnp
from jax import lax
from jax.experimental import pallas as pl
from jax.experimental.pallas import tpu as pltpu
from jax.sharding import PartitionSpec as P

BLK = 1024
QT = 64
H = 32
DH = 128
KB_DEV = 8
TASKS = 2
RIM = 3
SLOTS = 4
NT = 256
FACTOR = 1.0 / DH**0.5
MESH = pl.DeviceIdType.MESH
F32 = jnp.float32
BF16 = jnp.bfloat16


def lanes2(x):
    return jnp.concatenate([x, x], axis=1)


def kernel(
    slot_ref, doc_ref, w_ref, norm_ref, cot_ref, q_hbm, t_hbm, k_hbm,
    qg_hbm, wg_ref, kg_hbm,
    k_v, t_v, q_raw, q_h, qw_t, w_b, n_b, c_b, s_v, u_v, dk_v,
    rim_v, lend_v, lent_v, qg_v, kg_v,
    in_sem, rim_send, rim_recv, lend_send, lend_recv, out_sem,
):
    me = lax.axis_index("ctx")
    size = lax.axis_size("ctx")
    nxt = lax.rem(me + 1, size)
    prv = lax.rem(me + size - 1, size)
    base = me * (KB_DEV * BLK)

    load_q = pltpu.make_async_copy(q_hbm.at[0], q_raw, in_sem.at[0])
    loads = [
        pltpu.make_async_copy(
            k_hbm.at[0, pl.ds(b * BLK, BLK), :], k_v.at[RIM + b], in_sem.at[1 + b]
        )
        for b in range(KB_DEV)
    ]
    loads += [
        pltpu.make_async_copy(
            t_hbm.at[0, i, :, pl.ds(j * BLK, BLK)],
            t_v.at[i, j],
            in_sem.at[1 + KB_DEV + i * SLOTS + j],
        )
        for i in range(TASKS)
        for j in range(SLOTS)
    ]
    load_q.start()
    for load in loads:
        load.start()

    barrier = pltpu.get_barrier_semaphore()
    for other in (prv, nxt):
        pl.semaphore_signal(barrier, inc=1, device_id={"ctx": other}, device_id_type=MESH)
    pl.semaphore_wait(barrier, 2)

    def rim_copy(r):
        return pltpu.make_async_remote_copy(
            src_ref=k_hbm.at[0, pl.ds((KB_DEV - RIM + r) * BLK, BLK), :],
            dst_ref=rim_v.at[r],
            send_sem=rim_send.at[r],
            recv_sem=rim_recv.at[r],
            device_id={"ctx": nxt},
            device_id_type=MESH,
        )

    def lend_copy(r):
        return pltpu.make_async_remote_copy(
            src_ref=lend_v.at[r],
            dst_ref=lent_v.at[r],
            send_sem=lend_send.at[r],
            recv_sem=lend_recv.at[r],
            device_id={"ctx": prv},
            device_id_type=MESH,
        )

    for r in range(RIM):
        rim_copy(r).start()

    load_q.wait()
    for i in range(TASKS):
        w_all = w_ref[0, i] * FACTOR
        n_b[i] = jnp.broadcast_to(norm_ref[0, i : i + 1, :], (128, QT)).T
        c_b[i] = jnp.broadcast_to(cot_ref[0, i : i + 1, :], (128, QT)).T
        for pair in range(H // 2):
            parts = []
            for h in (2 * pair, 2 * pair + 1):
                wide = jnp.broadcast_to(w_all[:, h : h + 1], (QT, DH))
                rows = q_raw[i, :, h * DH : (h + 1) * DH]
                w_b[i, h * QT : (h + 1) * QT, :] = wide
                q_h[i, h * QT : (h + 1) * QT, :] = rows
                parts.append(rows.astype(F32) * wide)
            both = jnp.concatenate(parts, axis=0).astype(BF16)
            qw_t[i, :, pair * 128 : (pair + 1) * 128] = both.T

    def place(i, p):
        last = slot_ref[0, i] // (BLK // QT)
        if p is None:
            return last
        r = p - 1
        return last - 1 - lax.rem(last + 2 - r, 3)

    def process(i, p):
        diag = p is None
        block = place(i, p)
        query_first = slot_ref[0, i] * QT
        doc = doc_ref[0, i] - base
        first = (doc + SLOTS * BLK) // BLK - SLOTS
        column = jnp.clip(block - first, 0, SLOTS - 1)
        keys = k_v[RIM + block]
        keys_t = keys.T
        norm = lanes2(n_b[i])
        cot = lanes2(c_b[i])
        q_pos = lax.broadcasted_iota(jnp.int32, (QT, NT), 0) + query_first
        lane = lax.broadcasted_iota(jnp.int32, (QT, NT), 1)
        for n in range(BLK // NT):
            cols = slice(n * NT, (n + 1) * NT)
            index = jnp.zeros((QT, NT), F32)
            for pair in range(H // 2):
                s = jnp.dot(
                    q_h[i, pair * 128 : (pair + 1) * 128, :],
                    keys_t[:, cols],
                    preferred_element_type=F32,
                )
                s_v[pair * 128 : (pair + 1) * 128, cols] = s.astype(BF16)
                for e in range(2):
                    h = 2 * pair + e
                    w = lanes2(w_b[i, h * QT : (h + 1) * QT, :])
                    index += jnp.maximum(s[e * QT : (e + 1) * QT], 0.0) * w
            target = t_v[i, column, :, cols].astype(F32)
            k_pos = lane + (block * BLK + n * NT)
            live = (k_pos >= doc) & (k_pos <= q_pos)
            delta = jnp.where(live, cot * (jnp.exp(index - norm) - target), 0.0).astype(BF16)
            zero = jnp.zeros_like(delta)
            for h in range(H):
                rows = slice(h * QT, (h + 1) * QT)
                s_v[rows, cols] = jnp.where(s_v[rows, cols] > 0, delta, zero)
        u = jnp.dot(s_v[...], keys, preferred_element_type=F32)
        if diag:
            u_v[i] = u
        else:
            u_v[i] += u
        d_t = jnp.dot(qw_t[i], s_v[...], preferred_element_type=F32)
        dk_v[i, 0 if diag else p] = d_t.T

    for i in range(TASKS):
        dk_v[i, SLOTS] = jnp.zeros((BLK, DH), F32)
    for load in loads:
        load.wait()

    @pl.loop(0, TASKS)
    def _(i):
        process(i, None)

    @pl.loop(1, SLOTS)
    def _(p):
        rim_copy(p - 1).wait_recv()
        k_v[p - 1] = rim_v[p - 1]

        @pl.loop(0, TASKS)
        def _(i):
            process(i, p)

        total = jnp.zeros((BLK, DH), F32)
        for i in range(TASKS):
            total += dk_v[i, jnp.where(place(i, p) < 0, p, SLOTS)]
        lend_v[p - 1] = total.astype(BF16)
        lend_copy(p - 1).start()

    def own(b):
        total = jnp.zeros((BLK, DH), F32)
        for i in range(TASKS):
            last = place(i, None)
            inside = (b <= last) & (b >= last - RIM)
            p = jnp.where(last == b, 0, 1 + b % 3)
            total += dk_v[i, jnp.where(inside, p, SLOTS)]
        return total

    def key_out(lo, count, s):
        return pltpu.make_async_copy(
            kg_v.at[pl.ds(lo * BLK, count * BLK), :],
            kg_hbm.at[0, pl.ds(lo * BLK, count * BLK), :],
            out_sem.at[s],
        )

    for b in range(KB_DEV - RIM):
        kg_v[b * BLK : (b + 1) * BLK, :] = own(b).astype(BF16)
    key_out(0, KB_DEV - RIM, 0).start()

    for i in range(TASKS):
        sums = jnp.zeros((QT, 128), F32)
        lane = lax.broadcasted_iota(jnp.int32, (QT, 128), 1)
        for h in range(H):
            rows = slice(h * QT, (h + 1) * QT)
            u = u_v[i, rows, :]
            qg_v[i, :, h * DH : (h + 1) * DH] = (u * w_b[i, rows, :]).astype(BF16)
            dots = jnp.sum(u * q_h[i, rows, :].astype(F32), axis=1, keepdims=True)
            sums = jnp.where(lane == h, dots, sums)
        wg_ref[0, i] = sums[:, :H] * FACTOR
    query_out = pltpu.make_async_copy(qg_v, qg_hbm.at[0], out_sem.at[1])
    query_out.start()

    for r in range(RIM):
        lend_copy(r).wait_recv()
        b = KB_DEV - RIM + r
        kg_v[b * BLK : (b + 1) * BLK, :] = (own(b) + lent_v[r].astype(F32)).astype(BF16)
    key_out(KB_DEV - RIM, RIM, 2).start()

    for r in range(RIM):
        rim_copy(r).wait_send()
        lend_copy(r).wait_send()
    key_out(0, KB_DEV - RIM, 0).wait()
    query_out.wait()
    key_out(KB_DEV - RIM, RIM, 2).wait()


def local(queries, head_weights, key_vectors, targets, normalizers, loss_grad, tile_slot, doc_start):
    rows = H * QT
    vmem = pl.BlockSpec(memory_space=pltpu.VMEM)
    smem = pl.BlockSpec(memory_space=pltpu.SMEM)
    hbm = pl.BlockSpec(memory_space=pl.ANY)
    dma = pltpu.SemaphoreType.DMA
    return pl.pallas_call(
        kernel,
        out_shape=(
            jax.ShapeDtypeStruct(queries.shape, BF16),
            jax.ShapeDtypeStruct(head_weights.shape, F32),
            jax.ShapeDtypeStruct(key_vectors.shape, BF16),
        ),
        in_specs=[smem, smem, vmem, vmem, vmem, hbm, hbm, hbm],
        out_specs=(hbm, vmem, hbm),
        scratch_shapes=[
            pltpu.VMEM((RIM + KB_DEV, BLK, DH), BF16),
            pltpu.VMEM((TASKS, SLOTS, QT, BLK), BF16),
            pltpu.VMEM((TASKS, QT, H * DH), BF16),
            pltpu.VMEM((TASKS, rows, DH), BF16),
            pltpu.VMEM((TASKS, DH, rows), BF16),
            pltpu.VMEM((TASKS, rows, DH), F32),
            pltpu.VMEM((TASKS, QT, 128), F32),
            pltpu.VMEM((TASKS, QT, 128), F32),
            pltpu.VMEM((rows, BLK), BF16),
            pltpu.VMEM((TASKS, rows, DH), F32),
            pltpu.VMEM((TASKS, SLOTS + 1, BLK, DH), F32),
            pltpu.VMEM((RIM, BLK, DH), BF16),
            pltpu.VMEM((RIM, BLK, DH), BF16),
            pltpu.VMEM((RIM, BLK, DH), BF16),
            pltpu.VMEM((TASKS, QT, H * DH), BF16),
            pltpu.VMEM((KB_DEV * BLK, DH), BF16),
            dma((1 + KB_DEV + TASKS * SLOTS,)),
            dma((RIM,)),
            dma((RIM,)),
            dma((RIM,)),
            dma((RIM,)),
            dma((3,)),
        ],
        compiler_params=pltpu.CompilerParams(
            collective_id=0, has_side_effects=True, vmem_limit_bytes=60 << 20
        ),
    )(tile_slot, doc_start, head_weights, normalizers, loss_grad, queries, targets, key_vectors)


def solution(mesh):
    return jax.shard_map(
        local,
        mesh=mesh,
        in_specs=(
            P("sec", "ctx", None, None),
            P("sec", "ctx", None, None),
            P("sec", "ctx", None),
            P("sec", "ctx", None, None),
            P("sec", "ctx", None),
            P("sec", "ctx", None),
            P("sec", "ctx"),
            P("sec", "ctx"),
        ),
        out_specs=(P("sec", "ctx", None, None), P("sec", "ctx", None, None), P("sec", "ctx", None)),
        check_vma=False,
    )
```

```python
import jax
import jax.numpy as jnp
from jax import lax
from jax.experimental import pallas as pl
from jax.experimental.pallas import tpu as pltpu
from jax.sharding import PartitionSpec as P

BLK = 1024
QT = 64
H = 32
DH = 128
KB_DEV = 8
TASKS = 2
RIM = 3
SLOTS = 4
NT = 256
FACTOR = 1.0 / DH**0.5
MESH = pl.DeviceIdType.MESH
F32 = jnp.float32
BF16 = jnp.bfloat16


def lanes2(x):
    return jnp.concatenate([x, x], axis=1)


def kernel(
    slot_ref, doc_ref, w_ref, norm_ref, cot_ref, q_hbm, t_hbm, k_hbm,
    qg_v, wg_ref, kg_v,
    k_v, t_v, q_raw, q_h, qw_t, w_b, n_b, c_b, s_v, u_v, dk_v,
    rim_v, lend_v, lent_v,
    in_sem, rim_send, rim_recv, lend_send, lend_recv,
):
    me = lax.axis_index("ctx")
    size = lax.axis_size("ctx")
    nxt = lax.rem(me + 1, size)
    prv = lax.rem(me + size - 1, size)
    base = me * (KB_DEV * BLK)

    load_q = pltpu.make_async_copy(q_hbm.at[0], q_raw, in_sem.at[0])
    loads = [
        pltpu.make_async_copy(
            k_hbm.at[0, pl.ds(b * BLK, BLK), :], k_v.at[RIM + b], in_sem.at[1 + b]
        )
        for b in range(KB_DEV)
    ]
    loads += [
        pltpu.make_async_copy(
            t_hbm.at[0, i, :, pl.ds(j * BLK, BLK)],
            t_v.at[i, j],
            in_sem.at[1 + KB_DEV + i * SLOTS + j],
        )
        for i in range(TASKS)
        for j in range(SLOTS)
    ]
    load_q.start()
    for load in loads:
        load.start()

    barrier = pltpu.get_barrier_semaphore()
    for other in (prv, nxt):
        pl.semaphore_signal(barrier, inc=1, device_id={"ctx": other}, device_id_type=MESH)
    pl.semaphore_wait(barrier, 2)

    def rim_copy(r):
        return pltpu.make_async_remote_copy(
            src_ref=k_hbm.at[0, pl.ds((KB_DEV - RIM + r) * BLK, BLK), :],
            dst_ref=rim_v.at[r],
            send_sem=rim_send.at[r],
            recv_sem=rim_recv.at[r],
            device_id={"ctx": nxt},
            device_id_type=MESH,
        )

    def lend_copy(r):
        return pltpu.make_async_remote_copy(
            src_ref=lend_v.at[r],
            dst_ref=lent_v.at[r],
            send_sem=lend_send.at[r],
            recv_sem=lend_recv.at[r],
            device_id={"ctx": prv},
            device_id_type=MESH,
        )

    for r in range(RIM):
        rim_copy(r).start()

    load_q.wait()
    for i in range(TASKS):
        w_all = w_ref[0, i].T * FACTOR
        n_b[i][...] = jnp.broadcast_to(norm_ref[0, i : i + 1, :], (128, QT)).T
        c_b[i][...] = jnp.broadcast_to(cot_ref[0, i : i + 1, :], (128, QT)).T
        for pair in range(H // 2):
            parts = []
            for h in (2 * pair, 2 * pair + 1):
                wide = jnp.broadcast_to(w_all[:, h : h + 1], (QT, DH))
                rows = q_raw[i, :, h * DH : (h + 1) * DH]
                w_b[i][h * QT : (h + 1) * QT, :] = wide
                q_h[i][h * QT : (h + 1) * QT, :] = rows
                parts.append(rows.astype(F32) * wide)
            both = jnp.concatenate(parts, axis=0).astype(BF16)
            qw_t[i][:, pair * 128 : (pair + 1) * 128] = both.T

    def place(i, p):
        last = slot_ref[0, i] // (BLK // QT)
        return jnp.where(p == 0, last, last - 1 - lax.rem(last + 3 - p, 3))

    def process(i, p):
        block = place(i, p)
        query_first = slot_ref[0, i] * QT
        doc = doc_ref[0, i] - base
        first = (doc + SLOTS * BLK) // BLK - SLOTS
        column = jnp.clip(block - first, 0, SLOTS - 1)
        keys = k_v[RIM + block]
        keys_t = keys.T
        norm = lanes2(n_b[i][...])
        cot = lanes2(c_b[i][...])
        q_pos = lax.broadcasted_iota(jnp.int32, (QT, NT), 0) + query_first
        lane = lax.broadcasted_iota(jnp.int32, (QT, NT), 1)
        for n in range(BLK // NT):
            cols = slice(n * NT, (n + 1) * NT)
            index = jnp.zeros((QT, NT), F32)
            for pair in range(H // 2):
                s = jnp.dot(
                    q_h[i][pair * 128 : (pair + 1) * 128, :],
                    keys_t[:, cols],
                    preferred_element_type=F32,
                )
                s_v[pair * 128 : (pair + 1) * 128, cols] = s.astype(BF16)
                for e in range(2):
                    h = 2 * pair + e
                    w = lanes2(w_b[i][h * QT : (h + 1) * QT, :])
                    index += jnp.maximum(s[e * QT : (e + 1) * QT], 0.0) * w
            target = t_v[i, column, :, cols].astype(F32)
            k_pos = lane + (block * BLK + n * NT)
            live = (k_pos >= doc) & (k_pos <= q_pos)
            delta = jnp.where(live, cot * (jnp.exp(index - norm) - target), 0.0).astype(BF16)
            zero = jnp.zeros_like(delta)
            for h in range(H):
                rows = slice(h * QT, (h + 1) * QT)
                s_v[rows, cols] = jnp.where(s_v[rows, cols] > 0, delta, zero)
        u = jnp.dot(s_v[...], keys, preferred_element_type=F32)
        u_v[i][...] += u
        d_t = jnp.dot(qw_t[i][...], s_v[...], preferred_element_type=F32)
        dk_v[i][p] = d_t.T

    for i in range(TASKS):
        dk_v[i][SLOTS] = jnp.zeros((BLK, DH), F32)
        u_v[i][...] = jnp.zeros((H * QT, DH), F32)
    for load in loads:
        load.wait()

    @pl.loop(0, SLOTS)
    def _(p):
        @pl.when(p > 0)
        def _():
            rim_copy(p - 1).wait_recv()
            k_v[p - 1] = rim_v[p - 1]

        for i in range(TASKS):
            process(i, p)

        @pl.when(p > 0)
        def _():
            total = jnp.zeros((BLK, DH), F32)
            for i in range(TASKS):
                total += dk_v[i][jnp.where(place(i, p) < 0, p, SLOTS)]
            lend_v[p - 1] = total.astype(BF16)
            lend_copy(p - 1).start()

    def own(b):
        total = jnp.zeros((BLK, DH), F32)
        for i in range(TASKS):
            last = slot_ref[0, i] // (BLK // QT)
            inside = (b <= last) & (b >= last - RIM)
            p = jnp.where(last == b, 0, 1 + b % 3)
            total += dk_v[i][jnp.where(inside, p, SLOTS)]
        return total

    for b in range(KB_DEV - RIM):
        kg_v[0, b * BLK : (b + 1) * BLK, :] = own(b).astype(BF16)

    for i in range(TASKS):
        sums = jnp.zeros((QT, 128), F32)
        lane = lax.broadcasted_iota(jnp.int32, (QT, 128), 1)
        for h in range(H):
            rows = slice(h * QT, (h + 1) * QT)
            u = u_v[i][rows, :]
            qg_v[0, i, :, h * DH : (h + 1) * DH] = (u * w_b[i][rows, :]).astype(BF16)
            dots = jnp.sum(u * q_h[i][rows, :].astype(F32), axis=1, keepdims=True)
            sums = jnp.where(lane == h, dots, sums)
        wg_ref[0, i] = (sums * FACTOR).T[:H, :]

    for r in range(RIM):
        lend_copy(r).wait_recv()
        b = KB_DEV - RIM + r
        kg_v[0, b * BLK : (b + 1) * BLK, :] = (own(b) + lent_v[r].astype(F32)).astype(BF16)

    for r in range(RIM):
        rim_copy(r).wait_send()
        lend_copy(r).wait_send()


def write_out(*refs):
    copies = [
        pltpu.make_async_copy(refs[j], refs[3 + j], refs[6].at[j]) for j in range(3)
    ]
    for copy in copies:
        copy.start()
    for copy in copies:
        copy.wait()


def local(queries, head_weights, key_vectors, targets, normalizers, loss_grad, tile_slot, doc_start):
    rows = H * QT
    vmem = pl.BlockSpec(memory_space=pltpu.VMEM)
    smem = pl.BlockSpec(memory_space=pltpu.SMEM)
    hbm = pl.BlockSpec(memory_space=pltpu.HBM)
    dma = pltpu.SemaphoreType.DMA
    grads = pl.pallas_call(
        kernel,
        out_shape=(
            pltpu.VMEM(queries.shape, BF16),
            pltpu.VMEM((1, TASKS, H, QT), F32),
            pltpu.VMEM(key_vectors.shape, BF16),
        ),
        in_specs=[smem, smem, vmem, vmem, vmem, hbm, hbm, hbm],
        out_specs=(vmem, vmem, vmem),
        scratch_shapes=[
            pltpu.VMEM((RIM + KB_DEV, BLK, DH), BF16),
            pltpu.VMEM((TASKS, SLOTS, QT, BLK), BF16),
            pltpu.VMEM((TASKS, QT, H * DH), BF16),
            [pltpu.VMEM((rows, DH), BF16)] * TASKS,
            [pltpu.VMEM((DH, rows), BF16)] * TASKS,
            [pltpu.VMEM((rows, DH), F32)] * TASKS,
            [pltpu.VMEM((QT, 128), F32)] * TASKS,
            [pltpu.VMEM((QT, 128), F32)] * TASKS,
            pltpu.VMEM((rows, BLK), BF16),
            [pltpu.VMEM((rows, DH), F32)] * TASKS,
            [pltpu.VMEM((SLOTS + 1, BLK, DH), F32)] * TASKS,
            pltpu.VMEM((RIM, BLK, DH), BF16),
            pltpu.VMEM((RIM, BLK, DH), BF16),
            pltpu.VMEM((RIM, BLK, DH), BF16),
            dma((1 + KB_DEV + TASKS * SLOTS,)),
            dma((RIM,)),
            dma((RIM,)),
            dma((RIM,)),
            dma((RIM,)),
        ],
        compiler_params=pltpu.CompilerParams(
            collective_id=0, has_side_effects=True, vmem_limit_bytes=56 << 20
        ),
    )(
        tile_slot, doc_start, jnp.swapaxes(head_weights, 2, 3), normalizers, loss_grad,
        queries, targets, key_vectors,
    )
    query_grad, weight_grad, key_grad = pl.pallas_call(
        write_out,
        out_shape=[jax.ShapeDtypeStruct(g.shape, g.dtype) for g in grads],
        in_specs=[vmem] * 3,
        out_specs=[hbm] * 3,
        scratch_shapes=[dma((3,))],
        compiler_params=pltpu.CompilerParams(vmem_limit_bytes=1 << 20),
    )(*[pltpu.with_memory_space_constraint(g, pltpu.VMEM) for g in grads])
    return query_grad, jnp.swapaxes(weight_grad, 2, 3), key_grad


def solution(mesh):
    return jax.shard_map(
        local,
        mesh=mesh,
        in_specs=(
            P("sec", "ctx", None, None),
            P("sec", "ctx", None, None),
            P("sec", "ctx", None),
            P("sec", "ctx", None, None),
            P("sec", "ctx", None),
            P("sec", "ctx", None),
            P("sec", "ctx"),
            P("sec", "ctx"),
        ),
        out_specs=(P("sec", "ctx", None, None), P("sec", "ctx", None, None), P("sec", "ctx", None)),
        check_vma=False,
    )
```

```python
import jax
import jax.numpy as jnp
from jax import lax
from jax.experimental import pallas as pl
from jax.experimental.pallas import tpu as pltpu
from jax.sharding import PartitionSpec as P

BLK = 1024
QT = 64
H = 32
DH = 128
KB_DEV = 8
TASKS = 2
RIM = 3
SLOTS = 4
NT = 256
CUT = 2
PART = BLK // CUT
LENT = RIM * CUT
FACTOR = 1.0 / DH**0.5
MESH = pl.DeviceIdType.MESH
F32 = jnp.float32
BF16 = jnp.bfloat16


def lanes2(x):
    return jnp.concatenate([x, x], axis=1)


def kernel(
    slot_ref, doc_ref, w_ref, norm_ref, cot_ref, q_hbm, t_hbm, k_hbm,
    qg_v, wg_ref, kg_v,
    k_v, t_v, q_raw, q_h, qw_t, w_b, n_b, c_b, s_v, u_v, dk_v,
    rim_v, lend_v, lent_v,
    in_sem, rim_send, rim_recv, lend_send, lend_recv,
):
    me = lax.axis_index("ctx")
    size = lax.axis_size("ctx")
    nxt = jnp.minimum(me + 1, size - 1)
    prv = jnp.maximum(me - 1, 0)
    has_prev = me > 0
    has_next = me < size - 1
    base = me * (KB_DEV * BLK)

    load_q = pltpu.make_async_copy(q_hbm.at[0], q_raw, in_sem.at[0])
    loads = [
        pltpu.make_async_copy(
            k_hbm.at[0, pl.ds(b * PART, PART), :], k_v.at[LENT + b], in_sem.at[1 + b]
        )
        for b in range(KB_DEV * CUT)
    ]
    loads += [
        pltpu.make_async_copy(
            t_hbm.at[0, i, :, pl.ds(j * PART, PART)],
            t_v.at[i, j],
            in_sem.at[1 + CUT * (KB_DEV + i * SLOTS) + j],
        )
        for i in range(TASKS)
        for j in range(SLOTS * CUT)
    ]
    load_q.start()
    for load in loads:
        load.start()

    def rim_copy(r):
        return pltpu.make_async_remote_copy(
            src_ref=k_hbm.at[0, pl.ds((KB_DEV * CUT - LENT + r) * PART, PART), :],
            dst_ref=rim_v.at[r],
            send_sem=rim_send.at[r],
            recv_sem=rim_recv.at[r],
            device_id={"ctx": nxt},
            device_id_type=MESH,
        )

    def lend_copy(r):
        return pltpu.make_async_remote_copy(
            src_ref=lend_v.at[r],
            dst_ref=lent_v.at[r],
            send_sem=lend_send.at[r],
            recv_sem=lend_recv.at[r],
            device_id={"ctx": prv},
            device_id_type=MESH,
        )

    def prepare(i):
        w_all = w_ref[0, i].T * FACTOR
        n_b[i][...] = jnp.broadcast_to(norm_ref[0, i : i + 1, :], (128, QT)).T
        c_b[i][...] = jnp.broadcast_to(cot_ref[0, i : i + 1, :], (128, QT)).T
        for pair in range(H // 2):
            parts = []
            for h in (2 * pair, 2 * pair + 1):
                wide = jnp.broadcast_to(w_all[:, h : h + 1], (QT, DH))
                rows = q_raw[i, :, h * DH : (h + 1) * DH]
                w_b[i][h * QT : (h + 1) * QT, :] = wide
                q_h[i][h * QT : (h + 1) * QT, :] = rows
                parts.append(rows.astype(F32) * wide)
            both = jnp.concatenate(parts, axis=0).astype(BF16)
            qw_t[i][:, pair * 128 : (pair + 1) * 128] = both.T
        dk_v[i][SLOTS * CUT] = jnp.zeros((PART, DH), F32)
        u_v[i][...] = jnp.zeros((H * QT, DH), F32)

    barrier = pltpu.get_barrier_semaphore()

    @pl.when(has_prev)
    def _():
        pl.semaphore_signal(barrier, inc=1, device_id={"ctx": prv}, device_id_type=MESH)

    @pl.when(has_next)
    def _():
        pl.semaphore_signal(barrier, inc=1, device_id={"ctx": nxt}, device_id_type=MESH)

    pl.semaphore_wait(barrier, has_prev.astype(jnp.int32) + has_next.astype(jnp.int32))

    @pl.when(has_next)
    def _():
        for r in range(LENT):
            rim_copy(r).start()

    load_q.wait()
    for i in range(TASKS):
        prepare(i)

    def place(i, p):
        last = slot_ref[0, i] // (BLK // QT)
        return jnp.where(p == 0, last, last - 1 - lax.rem(last + 3 - p, 3))

    def mask_times_delta(i, p, c, keys):
        block = place(i, p)
        query_first = slot_ref[0, i] * QT
        doc = doc_ref[0, i] - base
        first = (doc + SLOTS * BLK) // BLK - SLOTS
        column = jnp.clip(block - first, 0, SLOTS - 1)
        keys_t = keys.T
        norm = lanes2(n_b[i][...])
        cot = lanes2(c_b[i][...])
        q_pos = lax.broadcasted_iota(jnp.int32, (QT, NT), 0) + query_first
        lane = lax.broadcasted_iota(jnp.int32, (QT, NT), 1)
        for n in range(PART // NT):
            cols = slice(n * NT, (n + 1) * NT)
            index = jnp.zeros((QT, NT), F32)
            for pair in range(H // 2):
                s = jnp.dot(
                    q_h[i][pair * 128 : (pair + 1) * 128, :],
                    keys_t[:, cols],
                    preferred_element_type=F32,
                )
                s_v[pair * 128 : (pair + 1) * 128, cols] = s.astype(BF16)
                for e in range(2):
                    h = 2 * pair + e
                    w = lanes2(w_b[i][h * QT : (h + 1) * QT, :])
                    index += jnp.maximum(s[e * QT : (e + 1) * QT], 0.0) * w
            target = t_v[i, column * CUT + c, :, cols].astype(F32)
            k_pos = lane + (block * BLK + c * PART + n * NT)
            live = (k_pos >= doc) & (k_pos <= q_pos)
            delta = jnp.where(live, cot * (jnp.exp(index - norm) - target), 0.0).astype(BF16)
            zero = jnp.zeros_like(delta)
            for h in range(H):
                rows = slice(h * QT, (h + 1) * QT)
                s_v[rows, cols] = jnp.where(s_v[rows, cols] > 0, delta, zero)

    def query_part(i, keys):
        u_v[i][...] += jnp.dot(s_v[...], keys, preferred_element_type=F32)

    def key_part(i, unit):
        d_t = jnp.dot(qw_t[i][...], s_v[...], preferred_element_type=F32)
        dk_v[i][unit] = d_t.T

    def lend(unit):
        p = unit // CUT
        total = jnp.zeros((PART, DH), F32)
        for i in range(TASKS):
            total += dk_v[i][jnp.where(place(i, p) < 0, unit, SLOTS * CUT)]
        lend_v[unit - CUT] = total.astype(BF16)

    def take_rim(r):
        @pl.when(has_prev)
        def _():
            rim_copy(r).wait_recv()
            k_v[r] = rim_v[r]

    @pl.when(jnp.logical_not(has_prev))
    def _():
        k_v[0:LENT] = jnp.zeros((LENT, PART, DH), BF16)

    for load in loads:
        load.wait()

    @pl.loop(0, SLOTS * CUT)
    def _(unit):
        p = unit // CUT
        c = unit % CUT

        @pl.when(p > 0)
        def _():
            take_rim(unit - CUT)

        for i in range(TASKS):
            keys = k_v[(RIM + place(i, p)) * CUT + c]
            mask_times_delta(i, p, c, keys)
            query_part(i, keys)
            key_part(i, unit)

        @pl.when((p > 0) & has_prev)
        def _():
            lend(unit)
            lend_copy(unit - CUT).start()

    def own(part):
        b, c = part // CUT, part % CUT
        total = jnp.zeros((PART, DH), F32)
        for i in range(TASKS):
            last = slot_ref[0, i] // (BLK // QT)
            inside = (b <= last) & (b >= last - RIM)
            p = jnp.where(last == b, 0, 1 + b % 3)
            total += dk_v[i][jnp.where(inside, p * CUT + c, SLOTS * CUT)]
        return total

    for part in range(KB_DEV * CUT - LENT):
        kg_v[0, part * PART : (part + 1) * PART, :] = own(part).astype(BF16)

    for i in range(TASKS):
        sums = jnp.zeros((QT, 128), F32)
        lane = lax.broadcasted_iota(jnp.int32, (QT, 128), 1)
        for h in range(H):
            rows = slice(h * QT, (h + 1) * QT)
            u = u_v[i][rows, :]
            qg_v[0, i, :, h * DH : (h + 1) * DH] = (u * w_b[i][rows, :]).astype(BF16)
            dots = jnp.sum(u * q_h[i][rows, :].astype(F32), axis=1, keepdims=True)
            sums = jnp.where(lane == h, dots, sums)
        wg_ref[0, i] = (sums * FACTOR).T[:H, :]

    @pl.when(has_next)
    def _():
        for r in range(LENT):
            lend_copy(r).wait_recv()

    @pl.when(jnp.logical_not(has_next))
    def _():
        lent_v[...] = jnp.zeros((LENT, PART, DH), BF16)

    for r in range(LENT):
        part = KB_DEV * CUT - LENT + r
        total = own(part) + lent_v[r].astype(F32)
        kg_v[0, part * PART : (part + 1) * PART, :] = total.astype(BF16)

    @pl.when(has_next)
    def _():
        for r in range(LENT):
            rim_copy(r).wait_send()

    @pl.when(has_prev)
    def _():
        for r in range(LENT):
            lend_copy(r).wait_send()


def write_out(*refs):
    copies = [
        pltpu.make_async_copy(refs[j], refs[3 + j], refs[6].at[j]) for j in range(3)
    ]
    for copy in copies:
        copy.start()
    for copy in copies:
        copy.wait()


def local(queries, head_weights, key_vectors, targets, normalizers, loss_grad, tile_slot, doc_start):
    rows = H * QT
    vmem = pl.BlockSpec(memory_space=pltpu.VMEM)
    smem = pl.BlockSpec(memory_space=pltpu.SMEM)
    hbm = pl.BlockSpec(memory_space=pltpu.HBM)
    dma = pltpu.SemaphoreType.DMA
    grads = pl.pallas_call(
        kernel,
        out_shape=(
            pltpu.VMEM(queries.shape, BF16),
            pltpu.VMEM((1, TASKS, H, QT), F32),
            pltpu.VMEM(key_vectors.shape, BF16),
        ),
        in_specs=[smem, smem, vmem, vmem, vmem, hbm, hbm, hbm],
        out_specs=(vmem, vmem, vmem),
        scratch_shapes=[
            pltpu.VMEM((LENT + KB_DEV * CUT, PART, DH), BF16),
            pltpu.VMEM((TASKS, SLOTS * CUT, QT, PART), BF16),
            pltpu.VMEM((TASKS, QT, H * DH), BF16),
            [pltpu.VMEM((rows, DH), BF16)] * TASKS,
            [pltpu.VMEM((DH, rows), BF16)] * TASKS,
            [pltpu.VMEM((rows, DH), F32)] * TASKS,
            [pltpu.VMEM((QT, 128), F32)] * TASKS,
            [pltpu.VMEM((QT, 128), F32)] * TASKS,
            pltpu.VMEM((rows, PART), BF16),
            [pltpu.VMEM((rows, DH), F32)] * TASKS,
            [pltpu.VMEM((SLOTS * CUT + 1, PART, DH), F32)] * TASKS,
            pltpu.VMEM((LENT, PART, DH), BF16),
            pltpu.VMEM((LENT, PART, DH), BF16),
            pltpu.VMEM((LENT, PART, DH), BF16),
            dma((1 + CUT * (KB_DEV + TASKS * SLOTS),)),
            dma((LENT,)),
            dma((LENT,)),
            dma((LENT,)),
            dma((LENT,)),
        ],
        compiler_params=pltpu.CompilerParams(
            collective_id=0, has_side_effects=True, vmem_limit_bytes=56 << 20
        ),
    )(
        tile_slot, doc_start, jnp.swapaxes(head_weights, 2, 3), normalizers, loss_grad,
        queries, targets, key_vectors,
    )
    query_grad, weight_grad, key_grad = pl.pallas_call(
        write_out,
        out_shape=[jax.ShapeDtypeStruct(g.shape, g.dtype) for g in grads],
        in_specs=[vmem] * 3,
        out_specs=[hbm] * 3,
        scratch_shapes=[dma((3,))],
        compiler_params=pltpu.CompilerParams(vmem_limit_bytes=1 << 20),
    )(*[pltpu.with_memory_space_constraint(g, pltpu.VMEM) for g in grads])
    return query_grad, jnp.swapaxes(weight_grad, 2, 3), key_grad


def solution(mesh):
    return jax.shard_map(
        local,
        mesh=mesh,
        in_specs=(
            P("sec", "ctx", None, None),
            P("sec", "ctx", None, None),
            P("sec", "ctx", None),
            P("sec", "ctx", None, None),
            P("sec", "ctx", None),
            P("sec", "ctx", None),
            P("sec", "ctx"),
            P("sec", "ctx"),
        ),
        out_specs=(P("sec", "ctx", None, None), P("sec", "ctx", None, None), P("sec", "ctx", None)),
        check_vma=False,
    )
```

```python
import jax
import jax.numpy as jnp
from jax import lax
from jax.experimental import pallas as pl
from jax.experimental.pallas import tpu as pltpu
from jax.sharding import PartitionSpec as P

BLK = 1024
QT = 64
H = 32
DH = 128
KB_DEV = 8
TASKS = 2
RIM = 3
SLOTS = 4
NT = 256
CUT = 1
PART = BLK // CUT
LENT = RIM * CUT
FACTOR = 1.0 / DH**0.5
MESH = pl.DeviceIdType.MESH
F32 = jnp.float32
BF16 = jnp.bfloat16


def lanes2(x):
    return jnp.concatenate([x, x], axis=1)


def kernel(
    slot_ref, doc_ref, w_ref, norm_ref, cot_ref, q_hbm, t_hbm, k_hbm,
    qg_v, wg_ref, kg_v,
    k_v, t_v, q_raw, q_h, qw_t, w_b, n_b, c_b, s_v, u_v, dk_v,
    rim_v, lend_v, lent_v,
    in_sem, rim_send, rim_recv, lend_send, lend_recv,
):
    me = lax.axis_index("ctx")
    size = lax.axis_size("ctx")
    nxt = jnp.minimum(me + 1, size - 1)
    prv = jnp.maximum(me - 1, 0)
    has_prev = me > 0
    has_next = me < size - 1
    base = me * (KB_DEV * BLK)

    load_q = pltpu.make_async_copy(q_hbm.at[0], q_raw, in_sem.at[0])
    loads = [
        pltpu.make_async_copy(
            k_hbm.at[0, pl.ds(b * PART, PART), :], k_v.at[LENT + b], in_sem.at[1 + b]
        )
        for b in range(KB_DEV * CUT)
    ]
    loads += [
        pltpu.make_async_copy(
            t_hbm.at[0, i, :, pl.ds(j * PART, PART)],
            t_v.at[i, j],
            in_sem.at[1 + CUT * (KB_DEV + i * SLOTS) + j],
        )
        for i in range(TASKS)
        for j in range(SLOTS * CUT)
    ]
    load_q.start()
    for load in loads:
        load.start()

    def rim_copy(r):
        return pltpu.make_async_remote_copy(
            src_ref=k_hbm.at[0, pl.ds((KB_DEV * CUT - LENT + r) * PART, PART), :],
            dst_ref=rim_v.at[r],
            send_sem=rim_send.at[r],
            recv_sem=rim_recv.at[r],
            device_id={"ctx": nxt},
            device_id_type=MESH,
        )

    def lend_copy(r):
        return pltpu.make_async_remote_copy(
            src_ref=lend_v.at[r],
            dst_ref=lent_v.at[r],
            send_sem=lend_send.at[r],
            recv_sem=lend_recv.at[r],
            device_id={"ctx": prv},
            device_id_type=MESH,
        )

    def prepare(i):
        w_all = w_ref[0, i].T * FACTOR
        n_b[i][...] = jnp.broadcast_to(norm_ref[0, i : i + 1, :], (128, QT)).T
        c_b[i][...] = jnp.broadcast_to(cot_ref[0, i : i + 1, :], (128, QT)).T
        for pair in range(H // 2):
            parts = []
            for h in (2 * pair, 2 * pair + 1):
                wide = jnp.broadcast_to(w_all[:, h : h + 1], (QT, DH))
                rows = q_raw[i, :, h * DH : (h + 1) * DH]
                w_b[i][h * QT : (h + 1) * QT, :] = wide
                q_h[i][h * QT : (h + 1) * QT, :] = rows
                parts.append(rows.astype(F32) * wide)
            both = jnp.concatenate(parts, axis=0).astype(BF16)
            qw_t[i][:, pair * 128 : (pair + 1) * 128] = both.T

    barrier = pltpu.get_barrier_semaphore()

    @pl.when(has_prev)
    def _():
        pl.semaphore_signal(barrier, inc=1, device_id={"ctx": prv}, device_id_type=MESH)

    @pl.when(has_next)
    def _():
        pl.semaphore_signal(barrier, inc=1, device_id={"ctx": nxt}, device_id_type=MESH)

    for i in range(TASKS):
        dk_v[i][SLOTS * CUT] = jnp.zeros((PART, DH), F32)
        u_v[i][...] = jnp.zeros((H * QT, DH), F32)

    @pl.when(jnp.logical_not(has_prev))
    def _():
        k_v[0:LENT] = jnp.zeros((LENT, PART, DH), BF16)

    pl.semaphore_wait(barrier, has_prev.astype(jnp.int32) + has_next.astype(jnp.int32))

    @pl.when(has_next)
    def _():
        for r in range(LENT):
            rim_copy(r).start()

    load_q.wait()
    for i in range(TASKS):
        prepare(i)

    def place(i, p):
        last = slot_ref[0, i] // (BLK // QT)
        return jnp.where(p == 0, last, last - 1 - lax.rem(last + 3 - p, 3))

    def mask_times_delta(i, p, c, keys):
        block = place(i, p)
        query_first = slot_ref[0, i] * QT
        doc = doc_ref[0, i] - base
        first = (doc + SLOTS * BLK) // BLK - SLOTS
        column = jnp.clip(block - first, 0, SLOTS - 1)
        keys_t = keys.T
        norm = lanes2(n_b[i][...])
        cot = lanes2(c_b[i][...])
        q_pos = lax.broadcasted_iota(jnp.int32, (QT, NT), 0) + query_first
        lane = lax.broadcasted_iota(jnp.int32, (QT, NT), 1)
        for n in range(PART // NT):
            cols = slice(n * NT, (n + 1) * NT)
            index = jnp.zeros((QT, NT), F32)
            for pair in range(H // 2):
                s = jnp.dot(
                    q_h[i][pair * 128 : (pair + 1) * 128, :],
                    keys_t[:, cols],
                    preferred_element_type=F32,
                )
                s_v[pair * 128 : (pair + 1) * 128, cols] = s.astype(BF16)
                for e in range(2):
                    h = 2 * pair + e
                    w = lanes2(w_b[i][h * QT : (h + 1) * QT, :])
                    index += jnp.maximum(s[e * QT : (e + 1) * QT], 0.0) * w
            target = t_v[i, column * CUT + c, :, cols].astype(F32)
            k_pos = lane + (block * BLK + c * PART + n * NT)
            live = (k_pos >= doc) & (k_pos <= q_pos)
            delta = jnp.where(live, cot * (jnp.exp(index - norm) - target), 0.0).astype(BF16)
            zero = jnp.zeros_like(delta)
            for h in range(H):
                rows = slice(h * QT, (h + 1) * QT)
                s_v[rows, cols] = jnp.where(s_v[rows, cols] > 0, delta, zero)

    def query_part(i, keys):
        u_v[i][...] += jnp.dot(s_v[...], keys, preferred_element_type=F32)

    def key_part(i, unit):
        d_t = jnp.dot(qw_t[i][...], s_v[...], preferred_element_type=F32)
        dk_v[i][unit] = d_t.T

    def lend(unit):
        p = unit // CUT
        total = jnp.zeros((PART, DH), F32)
        for i in range(TASKS):
            total += dk_v[i][jnp.where(place(i, p) < 0, unit, SLOTS * CUT)]
        lend_v[unit - CUT] = total.astype(BF16)

    def take_rim(r):
        @pl.when(has_prev)
        def _():
            rim_copy(r).wait_recv()
            k_v[r] = rim_v[r]

    for load in loads:
        load.wait()

    @pl.loop(0, SLOTS * CUT)
    def _(unit):
        p = unit // CUT
        c = unit % CUT

        @pl.when(p > 0)
        def _():
            take_rim(unit - CUT)

        for i in range(TASKS):
            keys = k_v[(RIM + place(i, p)) * CUT + c]
            mask_times_delta(i, p, c, keys)
            query_part(i, keys)
            key_part(i, unit)

        @pl.when((p > 0) & has_prev)
        def _():
            lend(unit)
            lend_copy(unit - CUT).start()

    def own(part):
        b, c = part // CUT, part % CUT
        total = jnp.zeros((PART, DH), F32)
        for i in range(TASKS):
            last = slot_ref[0, i] // (BLK // QT)
            inside = (b <= last) & (b >= last - RIM)
            p = jnp.where(last == b, 0, 1 + b % 3)
            total += dk_v[i][jnp.where(inside, p * CUT + c, SLOTS * CUT)]
        return total

    for part in range(KB_DEV * CUT - LENT):
        kg_v[0, part * PART : (part + 1) * PART, :] = own(part).astype(BF16)

    for i in range(TASKS):
        sums = jnp.zeros((QT, 128), F32)
        lane = lax.broadcasted_iota(jnp.int32, (QT, 128), 1)
        for h in range(H):
            rows = slice(h * QT, (h + 1) * QT)
            u = u_v[i][rows, :]
            qg_v[0, i, :, h * DH : (h + 1) * DH] = (u * w_b[i][rows, :]).astype(BF16)
            dots = jnp.sum(u * q_h[i][rows, :].astype(F32), axis=1, keepdims=True)
            sums = jnp.where(lane == h, dots, sums)
        wg_ref[0, i] = (sums * FACTOR).T[:H, :]

    @pl.when(has_next)
    def _():
        for r in range(LENT):
            lend_copy(r).wait_recv()

    @pl.when(jnp.logical_not(has_next))
    def _():
        lent_v[...] = jnp.zeros((LENT, PART, DH), BF16)

    for r in range(LENT):
        part = KB_DEV * CUT - LENT + r
        total = own(part) + lent_v[r].astype(F32)
        kg_v[0, part * PART : (part + 1) * PART, :] = total.astype(BF16)

    @pl.when(has_next)
    def _():
        for r in range(LENT):
            rim_copy(r).wait_send()

    @pl.when(has_prev)
    def _():
        for r in range(LENT):
            lend_copy(r).wait_send()


def write_out(query_v, weight_v, key_v, query_hbm, weight_hbm, key_hbm, sem):
    pairs = [(weight_v, weight_hbm)]
    pairs += [(query_v.at[0, i], query_hbm.at[0, i]) for i in range(TASKS)]
    for b in range(0, KB_DEV * BLK, 2 * BLK):
        rows = pl.ds(b, 2 * BLK)
        pairs.append((key_v.at[0, rows, :], key_hbm.at[0, rows, :]))
    copies = [pltpu.make_async_copy(*pair, sem.at[j]) for j, pair in enumerate(pairs)]
    for copy in copies:
        copy.start()
    for copy in copies:
        copy.wait()


def local(queries, head_weights, key_vectors, targets, normalizers, loss_grad, tile_slot, doc_start):
    rows = H * QT
    vmem = pl.BlockSpec(memory_space=pltpu.VMEM)
    smem = pl.BlockSpec(memory_space=pltpu.SMEM)
    hbm = pl.BlockSpec(memory_space=pltpu.HBM)
    dma = pltpu.SemaphoreType.DMA
    grads = pl.pallas_call(
        kernel,
        out_shape=(
            pltpu.VMEM(queries.shape, BF16),
            pltpu.VMEM((1, TASKS, H, QT), F32),
            pltpu.VMEM(key_vectors.shape, BF16),
        ),
        in_specs=[smem, smem, vmem, vmem, vmem, hbm, hbm, hbm],
        out_specs=(vmem, vmem, vmem),
        scratch_shapes=[
            pltpu.VMEM((LENT + KB_DEV * CUT, PART, DH), BF16),
            pltpu.VMEM((TASKS, SLOTS * CUT, QT, PART), BF16),
            pltpu.VMEM((TASKS, QT, H * DH), BF16),
            [pltpu.VMEM((rows, DH), BF16)] * TASKS,
            [pltpu.VMEM((DH, rows), BF16)] * TASKS,
            [pltpu.VMEM((rows, DH), F32)] * TASKS,
            [pltpu.VMEM((QT, 128), F32)] * TASKS,
            [pltpu.VMEM((QT, 128), F32)] * TASKS,
            pltpu.VMEM((rows, PART), BF16),
            [pltpu.VMEM((rows, DH), F32)] * TASKS,
            [pltpu.VMEM((SLOTS * CUT + 1, PART, DH), F32)] * TASKS,
            pltpu.VMEM((LENT, PART, DH), BF16),
            pltpu.VMEM((LENT, PART, DH), BF16),
            pltpu.VMEM((LENT, PART, DH), BF16),
            dma((1 + CUT * (KB_DEV + TASKS * SLOTS),)),
            dma((LENT,)),
            dma((LENT,)),
            dma((LENT,)),
            dma((LENT,)),
        ],
        compiler_params=pltpu.CompilerParams(
            collective_id=0, has_side_effects=True, vmem_limit_bytes=56 << 20
        ),
    )(
        tile_slot, doc_start, jnp.swapaxes(head_weights, 2, 3), normalizers, loss_grad,
        queries, targets, key_vectors,
    )
    query_grad, weight_grad, key_grad = pl.pallas_call(
        write_out,
        out_shape=[jax.ShapeDtypeStruct(g.shape, g.dtype) for g in grads],
        in_specs=[vmem] * 3,
        out_specs=[hbm] * 3,
        scratch_shapes=[dma((1 + TASKS + KB_DEV // 2,))],
        compiler_params=pltpu.CompilerParams(vmem_limit_bytes=1 << 20),
    )(*[pltpu.with_memory_space_constraint(g, pltpu.VMEM) for g in grads])
    return query_grad, jnp.swapaxes(weight_grad, 2, 3), key_grad


def solution(mesh):
    return jax.shard_map(
        local,
        mesh=mesh,
        in_specs=(
            P("sec", "ctx", None, None),
            P("sec", "ctx", None, None),
            P("sec", "ctx", None),
            P("sec", "ctx", None, None),
            P("sec", "ctx", None),
            P("sec", "ctx", None),
            P("sec", "ctx"),
            P("sec", "ctx"),
        ),
        out_specs=(P("sec", "ctx", None, None), P("sec", "ctx", None, None), P("sec", "ctx", None)),
        check_vma=False,
    )
```

```python
import jax
import jax.numpy as jnp
from jax import lax
from jax.experimental import pallas as pl
from jax.experimental.pallas import tpu as pltpu
from jax.sharding import PartitionSpec as P

BLK = 1024
QT = 64
H = 32
DH = 128
KB_DEV = 8
TASKS = 2
RIM = 3
SLOTS = 4
NT = 256
CUT = 1
PART = BLK // CUT
LENT = RIM * CUT
FACTOR = 1.0 / DH**0.5
MESH = pl.DeviceIdType.MESH
F32 = jnp.float32
BF16 = jnp.bfloat16


def lanes2(x):
    return jnp.concatenate([x, x], axis=1)


def kernel(
    slot_ref, doc_ref, w_ref, norm_ref, cot_ref, q_hbm, t_hbm, k_hbm,
    qg_v, wg_ref, kg_v,
    k_v, t_v, q_raw, q_h, qw_t, w_b, n_b, c_b, s_v, u_v, dk_v,
    rim_v, lend_v, lent_v,
    in_sem, rim_send, rim_recv, lend_send, lend_recv,
):
    me = lax.axis_index("ctx")
    size = lax.axis_size("ctx")
    nxt = jnp.minimum(me + 1, size - 1)
    prv = jnp.maximum(me - 1, 0)
    has_prev = me > 0
    has_next = me < size - 1
    base = me * (KB_DEV * BLK)

    load_q = pltpu.make_async_copy(q_hbm.at[0], q_raw, in_sem.at[0])
    loads = [
        pltpu.make_async_copy(
            k_hbm.at[0, pl.ds(b * PART, PART), :], k_v.at[LENT + b], in_sem.at[1 + b]
        )
        for b in range(KB_DEV * CUT)
    ]
    loads += [
        pltpu.make_async_copy(
            t_hbm.at[0, i, :, pl.ds(j * PART, PART)],
            t_v.at[i, j],
            in_sem.at[1 + CUT * (KB_DEV + i * SLOTS) + j],
        )
        for i in range(TASKS)
        for j in range(SLOTS * CUT)
    ]
    load_q.start()
    for load in loads:
        load.start()

    def rim_copy(r):
        return pltpu.make_async_remote_copy(
            src_ref=k_hbm.at[0, pl.ds((KB_DEV * CUT - LENT + r) * PART, PART), :],
            dst_ref=rim_v.at[r],
            send_sem=rim_send.at[r],
            recv_sem=rim_recv.at[r],
            device_id={"ctx": nxt},
            device_id_type=MESH,
        )

    def lend_copy(r):
        return pltpu.make_async_remote_copy(
            src_ref=lend_v.at[r],
            dst_ref=lent_v.at[r],
            send_sem=lend_send.at[r],
            recv_sem=lend_recv.at[r],
            device_id={"ctx": prv},
            device_id_type=MESH,
        )

    def prepare(i):
        w_all = w_ref[0, i].T * FACTOR
        n_b[i][...] = jnp.broadcast_to(norm_ref[0, i : i + 1, :], (128, QT)).T
        c_b[i][...] = jnp.broadcast_to(cot_ref[0, i : i + 1, :], (128, QT)).T
        for pair in range(H // 2):
            parts = []
            for h in (2 * pair, 2 * pair + 1):
                wide = jnp.broadcast_to(w_all[:, h : h + 1], (QT, DH))
                rows = q_raw[i, :, h * DH : (h + 1) * DH]
                w_b[i][h * QT : (h + 1) * QT, :] = wide
                q_h[i][h * QT : (h + 1) * QT, :] = rows
                parts.append(rows.astype(F32) * wide)
            both = jnp.concatenate(parts, axis=0).astype(BF16)
            qw_t[i][:, pair * 128 : (pair + 1) * 128] = both.T

    barrier = pltpu.get_barrier_semaphore()

    @pl.when(has_prev)
    def _():
        pl.semaphore_signal(barrier, inc=1, device_id={"ctx": prv}, device_id_type=MESH)

    @pl.when(has_next)
    def _():
        pl.semaphore_signal(barrier, inc=1, device_id={"ctx": nxt}, device_id_type=MESH)

    for i in range(TASKS):
        dk_v[i][SLOTS * CUT] = jnp.zeros((PART, DH), F32)
        u_v[i][...] = jnp.zeros((H * QT, DH), F32)

    @pl.when(jnp.logical_not(has_prev))
    def _():
        k_v[0:LENT] = jnp.zeros((LENT, PART, DH), BF16)

    load_q.wait()
    prepare(0)
    pl.semaphore_wait(barrier, has_prev.astype(jnp.int32) + has_next.astype(jnp.int32))

    @pl.when(has_next)
    def _():
        for r in range(LENT):
            rim_copy(r).start()

    prepare(1)

    def place(i, p):
        last = slot_ref[0, i] // (BLK // QT)
        return jnp.where(p == 0, last, last - 1 - lax.rem(last + 3 - p, 3))

    def mask_times_delta(i, p, c, keys):
        block = place(i, p)
        query_first = slot_ref[0, i] * QT
        doc = doc_ref[0, i] - base
        first = (doc + SLOTS * BLK) // BLK - SLOTS
        column = jnp.clip(block - first, 0, SLOTS - 1)
        keys_t = keys.T
        norm = lanes2(n_b[i][...])
        cot = lanes2(c_b[i][...])
        q_pos = lax.broadcasted_iota(jnp.int32, (QT, NT), 0) + query_first
        lane = lax.broadcasted_iota(jnp.int32, (QT, NT), 1)
        for n in range(PART // NT):
            cols = slice(n * NT, (n + 1) * NT)
            index = jnp.zeros((QT, NT), F32)
            for pair in range(H // 2):
                s = jnp.dot(
                    q_h[i][pair * 128 : (pair + 1) * 128, :],
                    keys_t[:, cols],
                    preferred_element_type=F32,
                )
                s_v[pair * 128 : (pair + 1) * 128, cols] = s.astype(BF16)
                for e in range(2):
                    h = 2 * pair + e
                    w = lanes2(w_b[i][h * QT : (h + 1) * QT, :])
                    index += jnp.maximum(s[e * QT : (e + 1) * QT], 0.0) * w
            target = t_v[i, column * CUT + c, :, cols].astype(F32)
            k_pos = lane + (block * BLK + c * PART + n * NT)
            live = (k_pos >= doc) & (k_pos <= q_pos)
            delta = jnp.where(live, cot * (jnp.exp(index - norm) - target), 0.0).astype(BF16)
            zero = jnp.zeros_like(delta)
            for h in range(H):
                rows = slice(h * QT, (h + 1) * QT)
                s_v[rows, cols] = jnp.where(s_v[rows, cols] > 0, delta, zero)

    def query_part(i, keys):
        u_v[i][...] += jnp.dot(s_v[...], keys, preferred_element_type=F32)

    def key_part(i, unit):
        d_t = jnp.dot(qw_t[i][...], s_v[...], preferred_element_type=F32)
        dk_v[i][unit] = d_t.T

    def lend(unit):
        p = unit // CUT
        total = jnp.zeros((PART, DH), F32)
        for i in range(TASKS):
            total += dk_v[i][jnp.where(place(i, p) < 0, unit, SLOTS * CUT)]
        lend_v[unit - CUT] = total.astype(BF16)

    def take_rim(r):
        @pl.when(has_prev)
        def _():
            rim_copy(r).wait_recv()
            k_v[r] = rim_v[r]

    for load in loads:
        load.wait()

    @pl.loop(0, SLOTS * CUT)
    def _(unit):
        p = unit // CUT
        c = unit % CUT

        @pl.when(p > 0)
        def _():
            take_rim(unit - CUT)

        for i in range(TASKS):
            keys = k_v[(RIM + place(i, p)) * CUT + c]
            mask_times_delta(i, p, c, keys)
            query_part(i, keys)
            key_part(i, unit)

        @pl.when((p > 0) & has_prev)
        def _():
            lend(unit)
            lend_copy(unit - CUT).start()

    def own(part):
        b, c = part // CUT, part % CUT
        total = jnp.zeros((PART, DH), F32)
        for i in range(TASKS):
            last = slot_ref[0, i] // (BLK // QT)
            inside = (b <= last) & (b >= last - RIM)
            p = jnp.where(last == b, 0, 1 + b % 3)
            total += dk_v[i][jnp.where(inside, p * CUT + c, SLOTS * CUT)]
        return total

    for part in range(KB_DEV * CUT - LENT):
        kg_v[0, part * PART : (part + 1) * PART, :] = own(part).astype(BF16)

    for i in range(TASKS):
        sums = jnp.zeros((QT, 128), F32)
        lane = lax.broadcasted_iota(jnp.int32, (QT, 128), 1)
        for h in range(H):
            rows = slice(h * QT, (h + 1) * QT)
            u = u_v[i][rows, :]
            qg_v[0, i, :, h * DH : (h + 1) * DH] = (u * w_b[i][rows, :]).astype(BF16)
            dots = jnp.sum(u * q_h[i][rows, :].astype(F32), axis=1, keepdims=True)
            sums = jnp.where(lane == h, dots, sums)
        wg_ref[0, i] = (sums * FACTOR).T[:H, :]

    @pl.when(has_next)
    def _():
        for r in range(LENT):
            lend_copy(r).wait_recv()

    @pl.when(jnp.logical_not(has_next))
    def _():
        lent_v[...] = jnp.zeros((LENT, PART, DH), BF16)

    for r in range(LENT):
        part = KB_DEV * CUT - LENT + r
        total = own(part) + lent_v[r].astype(F32)
        kg_v[0, part * PART : (part + 1) * PART, :] = total.astype(BF16)

    @pl.when(has_next)
    def _():
        for r in range(LENT):
            rim_copy(r).wait_send()

    @pl.when(has_prev)
    def _():
        for r in range(LENT):
            lend_copy(r).wait_send()


def write_out(query_v, weight_v, key_v, query_hbm, weight_hbm, key_hbm, sem):
    pairs = [(weight_v, weight_hbm)]
    pairs += [(query_v.at[0, i], query_hbm.at[0, i]) for i in range(TASKS)]
    for b in range(0, KB_DEV * BLK, 2 * BLK):
        rows = pl.ds(b, 2 * BLK)
        pairs.append((key_v.at[0, rows, :], key_hbm.at[0, rows, :]))
    copies = [pltpu.make_async_copy(*pair, sem.at[j]) for j, pair in enumerate(pairs)]
    for copy in copies:
        copy.start()
    for copy in copies:
        copy.wait()


def local(queries, head_weights, key_vectors, targets, normalizers, loss_grad, tile_slot, doc_start):
    rows = H * QT
    vmem = pl.BlockSpec(memory_space=pltpu.VMEM)
    smem = pl.BlockSpec(memory_space=pltpu.SMEM)
    hbm = pl.BlockSpec(memory_space=pltpu.HBM)
    dma = pltpu.SemaphoreType.DMA
    grads = pl.pallas_call(
        kernel,
        out_shape=(
            pltpu.VMEM(queries.shape, BF16),
            pltpu.VMEM((1, TASKS, H, QT), F32),
            pltpu.VMEM(key_vectors.shape, BF16),
        ),
        in_specs=[smem, smem, vmem, vmem, vmem, hbm, hbm, hbm],
        out_specs=(vmem, vmem, vmem),
        scratch_shapes=[
            pltpu.VMEM((LENT + KB_DEV * CUT, PART, DH), BF16),
            pltpu.VMEM((TASKS, SLOTS * CUT, QT, PART), BF16),
            pltpu.VMEM((TASKS, QT, H * DH), BF16),
            [pltpu.VMEM((rows, DH), BF16)] * TASKS,
            [pltpu.VMEM((DH, rows), BF16)] * TASKS,
            [pltpu.VMEM((rows, DH), F32)] * TASKS,
            [pltpu.VMEM((QT, 128), F32)] * TASKS,
            [pltpu.VMEM((QT, 128), F32)] * TASKS,
            pltpu.VMEM((rows, PART), BF16),
            [pltpu.VMEM((rows, DH), F32)] * TASKS,
            [pltpu.VMEM((SLOTS * CUT + 1, PART, DH), F32)] * TASKS,
            pltpu.VMEM((LENT, PART, DH), BF16),
            pltpu.VMEM((LENT, PART, DH), BF16),
            pltpu.VMEM((LENT, PART, DH), BF16),
            dma((1 + CUT * (KB_DEV + TASKS * SLOTS),)),
            dma((LENT,)),
            dma((LENT,)),
            dma((LENT,)),
            dma((LENT,)),
        ],
        compiler_params=pltpu.CompilerParams(
            collective_id=0, has_side_effects=True, vmem_limit_bytes=56 << 20
        ),
    )(
        tile_slot, doc_start, jnp.swapaxes(head_weights, 2, 3), normalizers, loss_grad,
        queries, targets, key_vectors,
    )
    query_grad, weight_grad, key_grad = pl.pallas_call(
        write_out,
        out_shape=[jax.ShapeDtypeStruct(g.shape, g.dtype) for g in grads],
        in_specs=[vmem] * 3,
        out_specs=[hbm] * 3,
        scratch_shapes=[dma((1 + TASKS + KB_DEV // 2,))],
        compiler_params=pltpu.CompilerParams(vmem_limit_bytes=1 << 20),
    )(*[pltpu.with_memory_space_constraint(g, pltpu.VMEM) for g in grads])
    return query_grad, jnp.swapaxes(weight_grad, 2, 3), key_grad


def solution(mesh):
    return jax.shard_map(
        local,
        mesh=mesh,
        in_specs=(
            P("sec", "ctx", None, None),
            P("sec", "ctx", None, None),
            P("sec", "ctx", None),
            P("sec", "ctx", None, None),
            P("sec", "ctx", None),
            P("sec", "ctx", None),
            P("sec", "ctx"),
            P("sec", "ctx"),
        ),
        out_specs=(P("sec", "ctx", None, None), P("sec", "ctx", None, None), P("sec", "ctx", None)),
        check_vma=False,
    )
```
